32 devices in a mesh: ctx: 8 (over z, x), head: 4 (over y, core).
Axes of the slice: x: 2, y: 2, z: 4, core: 2. Of those that a mesh axis runs over, the one named last changes fastest.
Arguments:
- channels_in: bfloat16 [12288, 8192], P('ctx', 'head'), may hold values from -6 to 6
- state_maps: bfloat16 [12288, 2, 1024], P('ctx', None, 'head'), may hold values from -6 to 6
- gate_in: bfloat16 [12288, 8192], P('ctx', 'head'), may hold values from -6 to 6
- step_raw: float32 [12288, 128], P('ctx', 'head'), may hold values from -1.2 to 80
- convolution_channel_taps: float32 [4, 8192], P(None, 'head'), may hold values from -3 to 3
- conv_maps: float32 [4, 2, 1024], P(None, None, 'head'), may hold values from -3 to 3
- head_rates: float32 [2, 128], P(None, 'head'), may hold values from -8 to 0
- skip_gain: float32 [128], P('head'), may hold values from 0.5 to 2
- norm_gain: float32 [8192], P('head'), may hold values from 0.5 to 1.5
Outputs:
- relaid: bfloat16 [12288, 8192], P(('ctx', 'head'))
The draws below stay inside these ranges and needn't reach their ends.
All inputs are finite; a program needn't handle non-finite values.
Results may differ from the reference program's by a relative error of at most 0.006.
Values may be sent and summed in bfloat16 or wider, within the bound.
No kernel may reach another device: no remote copies, remote signals or barrier semaphores. Data moves between devices by JAX's collectives and lax.ppermute only.
A program may use at most 192 MiB of HBM per device.

```python
import jax
import jax.numpy as jnp
from jax import lax

HEADS = 128
HEAD_DIM = 64
STATE = 128
GROUPS = 8
TAPS = 4
STRETCH = 256
LARGE_STEP_COUNT = 6
D_INNER = 8192
SEQUENCE_LENGTH = 12288


def large_step_rows(key):
    return jax.random.randint(jax.random.fold_in(key, 4711), (LARGE_STEP_COUNT,), 0, SEQUENCE_LENGTH)


def draw_channels_in(key, part):
    noise_key = jax.random.fold_in(key, 11)
    noise = jnp.clip(jax.random.normal(noise_key, (SEQUENCE_LENGTH, D_INNER), jnp.float32), -6.0, 6.0)
    sequence_positions = jnp.arange(SEQUENCE_LENGTH, dtype=jnp.int32)[:, None]
    position_distance = sequence_positions - large_step_rows(key)[None, :]
    nearby = jnp.any((position_distance >= 0) & (position_distance < TAPS), axis=1)
    factor = jnp.where(nearby, 0.02, 1.0)
    return (noise * factor[:, None]).astype(jnp.bfloat16)


def draw_step_raw(key, part):
    noise = jax.random.uniform(jax.random.fold_in(key, 21), (SEQUENCE_LENGTH, HEADS), jnp.float32, -0.7, 0.7)
    blocks = jax.random.uniform(jax.random.fold_in(key, 22), (SEQUENCE_LENGTH // STRETCH, 1, HEADS), jnp.float32, -0.5, 0.5)
    shifted = (noise.reshape(SEQUENCE_LENGTH // STRETCH, STRETCH, HEADS) + blocks).reshape(SEQUENCE_LENGTH, HEADS)
    large_step_mask = jnp.any(jnp.arange(SEQUENCE_LENGTH, dtype=jnp.int32)[:, None] == large_step_rows(key)[None, :], axis=1)
    return jnp.where(large_step_mask[:, None], 80.0, shifted).astype(jnp.float32)


def draw_head_rates(key, part):
    ranking = jax.random.permutation(jax.random.fold_in(key, 31), HEADS)
    quick_share = HEADS // 2
    quick = ranking < quick_share
    spread = jax.random.uniform(jax.random.fold_in(key, 32), (2, HEADS), jnp.float32)
    half_log = 0.5 * jnp.log(jnp.float32(SEQUENCE_LENGTH))
    slow_bias = -half_log - 0.3 + 0.6 * spread[0]
    quick_bias = -1.8 + 0.6 * spread[0]
    slow_rate = -half_log + jnp.log(0.5) + jnp.log(3.0) * spread[1]
    quick_rate = jnp.log(0.1) + jnp.log(1.667) * spread[1]
    return jnp.stack([jnp.where(quick, quick_bias, slow_bias), jnp.where(quick, quick_rate, slow_rate)]).astype(jnp.float32)


def block_scale(own_key, extent, shards, smallest, high):
    factor_of, own = 1.0, jax.random.fold_in(own_key, 6)
    for dim, parts in shards:
        heights = jnp.exp(jax.random.uniform(jax.random.fold_in(own, dim), (parts,), jnp.float32, smallest / len(shards), high / len(shards)))
        factor_of = factor_of * jnp.repeat(heights, extent[dim] // parts).reshape([-1 if axis == dim else 1 for axis in range(len(extent))])
    return factor_of


def normal_values(stream_key, dims, scale, reach, shards=(), held_as=jnp.bfloat16):
    values = scale * jax.random.normal(stream_key, dims, jnp.float32)
    if shards:
        values = values * block_scale(stream_key, dims, shards, -0.22, 0.18)
    return jnp.clip(values, -reach, reach).astype(held_as)


def setup_inputs(seed: int = 0) -> dict:
    seeds = jax.random.split(jax.random.key(seed), 10)
    return {
        "channels_in": draw_channels_in(jax.random.fold_in(seeds[9], 71), 0),
        "state_maps": normal_values(seeds[1], (SEQUENCE_LENGTH, 2, GROUPS * STATE), 1.0, 6.0, ((0, 8), (2, 4))),
        "gate_in": normal_values(seeds[2], (SEQUENCE_LENGTH, D_INNER), 1.0, 6.0, ((0, 8), (1, 4))),
        "step_raw": draw_step_raw(jax.random.fold_in(seeds[9], 71), 0),
        "convolution_channel_taps": normal_values(seeds[4], (TAPS, D_INNER), TAPS ** -0.5, 3.0, ((1, 4),), jnp.float32),
        "conv_maps": normal_values(seeds[5], (TAPS, 2, GROUPS * STATE), TAPS ** -0.5, 3.0, ((2, 4),), jnp.float32),
        "head_rates": draw_head_rates(jax.random.fold_in(seeds[9], 71), 0),
        "skip_gain": jnp.clip(0.5 + 1.5 * jax.random.uniform(seeds[7], (HEADS,), jnp.float32) ** block_scale(seeds[7], (HEADS,), ((0, 4),), -0.2, 0.2), 0.5, 2.0),
        "norm_gain": jnp.clip(1.0 + 0.1 * jax.random.normal(seeds[8], (D_INNER,), jnp.float32), 0.5, 1.5),
    }


HIGHEST_PRECISION = lax.Precision.HIGHEST
EPSILON = 1e-05

def conv_silu(sequence, kernel):
    padded = jnp.concatenate([jnp.zeros((TAPS - 1,) + sequence.shape[1:], jnp.float32), sequence.astype(jnp.float32)], 0)
    summed = jnp.zeros(sequence.shape, jnp.float32)
    for offset in range(TAPS):
        summed = summed + kernel[offset] * padded[offset:offset + SEQUENCE_LENGTH]
    return jax.nn.silu(summed).astype(jnp.bfloat16)

def stretch_terms(pieces):
    values, b_maps, c_maps, step_sizes, log_rates = pieces
    length = values.shape[0]
    cumlog = jnp.cumsum(log_rates, axis=0)
    causal = jnp.arange(length)[:, None] >= jnp.arange(length)[None, :]
    log_gaps = cumlog[:, None] - cumlog[None, :]
    decays = jnp.exp(jnp.where(causal[:, :, None, None], log_gaps, -jnp.inf))
    scores = jnp.einsum('tgn,sgn->tsg', c_maps, b_maps, preferred_element_type=jnp.float32)
    weights = (scores[..., None] * decays * step_sizes[None]).astype(jnp.bfloat16)
    values_wide = values.astype(jnp.float32)
    inside = jnp.einsum('tsgh,sghp->tghp', weights.astype(jnp.float32), values_wide, precision=HIGHEST_PRECISION)
    tail_weights = jnp.exp(cumlog[-1][None] - cumlog) * step_sizes
    tail = (tail_weights[..., None] * values_wide).astype(jnp.bfloat16)
    b_wide = b_maps.astype(jnp.float32)
    summary = jnp.einsum('sghp,sgn->ghpn', tail.astype(jnp.float32), b_wide, precision=HIGHEST_PRECISION)
    return (inside, summary, cumlog)

def reference(channels_in, state_maps, gate_in, step_raw, convolution_channel_taps, conv_maps, head_rates, skip_gain, norm_gain):
    conv_x = conv_silu(channels_in, convolution_channel_taps)
    conv_bc = conv_silu(state_maps, conv_maps)
    step_sizes = jax.nn.softplus(step_raw + head_rates[0][None, :])
    log_rates = -jnp.exp(head_rates[1])[None, :] * step_sizes
    stretch_count = SEQUENCE_LENGTH // STRETCH
    per_group = HEADS // GROUPS
    values = conv_x.reshape(stretch_count, STRETCH, GROUPS, per_group, HEAD_DIM)
    b_maps = conv_bc[:, 0].reshape(stretch_count, STRETCH, GROUPS, STATE)
    c_maps = conv_bc[:, 1].reshape(stretch_count, STRETCH, GROUPS, STATE)
    step_sizes = step_sizes.reshape(stretch_count, STRETCH, GROUPS, per_group)
    log_rates = log_rates.reshape(stretch_count, STRETCH, GROUPS, per_group)

    def advance(carried, pieces):
        inside, summary, cumlog = stretch_terms(pieces)
        c_block = pieces[2].astype(jnp.float32)
        from_state = jnp.einsum('tgn,ghpn->tghp', c_block, carried, precision=HIGHEST_PRECISION) * jnp.exp(cumlog)[..., None]
        renewed = jnp.exp(cumlog[-1])[..., None, None] * carried + summary
        return (renewed, inside + from_state)
    initial = jnp.zeros((GROUPS, per_group, HEAD_DIM, STATE), jnp.float32)
    final_state, outputs = lax.scan(advance, initial, (values, b_maps, c_maps, step_sizes, log_rates))
    skipped = skip_gain.reshape(GROUPS, per_group)[..., None] * values.astype(jnp.float32)
    ssm_out = (outputs + skipped).reshape(SEQUENCE_LENGTH, GROUPS, per_group * HEAD_DIM)
    gating = jax.nn.silu(gate_in.astype(jnp.float32)).reshape(SEQUENCE_LENGTH, GROUPS, per_group * HEAD_DIM)
    gated_out = ssm_out * gating
    inverse_rms = lax.rsqrt(lax.optimization_barrier(jnp.mean(gated_out * gated_out, axis=-1, keepdims=True)) + EPSILON)
    normed = gated_out * inverse_rms * norm_gain.reshape(GROUPS, per_group * HEAD_DIM)
    return normed.reshape(SEQUENCE_LENGTH, HEADS * HEAD_DIM).astype(jnp.bfloat16)
```

```python
import functools
import math

import jax
import jax.numpy as jnp
from jax import lax
from jax.experimental import pallas as pl
from jax.experimental.pallas import tpu as pltpu
from jax.sharding import PartitionSpec as P

HEAD_DIM = 64
STATE = 128
TAPS = 4
LANES = 128
EPSILON = 1e-05
LOG2E = 1.0 / math.log(2.0)
HIGHEST = lax.Precision.HIGHEST
F32 = jnp.float32
BF16 = jnp.bfloat16
VMEM_LIMIT = 60 * 1024 * 1024


def dot(a, b, dims=((1,), (0,)), precision=None):
    return lax.dot_general(a, b, (dims, ((), ())), precision=precision, preferred_element_type=F32)


def silu(v):
    return v / (1.0 + jnp.exp(-v))


def params(n_dims):
    return pltpu.CompilerParams(
        dimension_semantics=("arbitrary",) * n_dims, vmem_limit_bytes=VMEM_LIMIT
    )


def cost(flops, bytes_accessed, transcendentals=0):
    return pl.CostEstimate(
        flops=int(flops), bytes_accessed=int(bytes_accessed), transcendentals=int(transcendentals)
    )


def prep_kernel(q, step_ref, rates_ref, cum_ref, rel_ref, rel_t_ref, before_ref):
    rows, heads = step_ref.shape
    lower = (
        lax.broadcasted_iota(jnp.int32, (q, q), 0) >= lax.broadcasted_iota(jnp.int32, (q, q), 1)
    ).astype(F32)
    bias = rates_ref[0:1, :]
    rate = -jnp.exp(rates_ref[1:2, :]) * LOG2E
    before = jnp.zeros((1, heads), F32)
    for k in range(rows // q):
        raw = step_ref[k * q : (k + 1) * q, :] + bias
        step = jnp.maximum(raw, 0.0) + jnp.log1p(jnp.exp(-jnp.abs(raw)))
        cum = dot(lower, rate * step, precision=HIGHEST)
        rel = cum - jnp.log(step) * LOG2E
        cum_ref[k * q : (k + 1) * q, :] = cum
        rel_ref[k * q : (k + 1) * q, :] = rel
        rel_t_ref[k] = jnp.transpose(rel)
        before_ref[k : k + 1, :] = before
        before = before + cum[q - 1 : q, :]
    before_ref[rows // q : rows // q + 1, :] = before


def prep(step_raw, head_rates, q):
    rows, heads = step_raw.shape
    blocks = rows // q
    return pl.pallas_call(
        functools.partial(prep_kernel, q),
        out_shape=(
            jax.ShapeDtypeStruct((rows, heads), F32),
            jax.ShapeDtypeStruct((rows, heads), F32),
            jax.ShapeDtypeStruct((blocks, heads, q), F32),
            jax.ShapeDtypeStruct((blocks + 1, heads), F32),
        ),
        compiler_params=pltpu.CompilerParams(vmem_limit_bytes=VMEM_LIMIT),
        cost_estimate=cost(rows * q * heads * 12, rows * heads * 16, rows * heads * 4),
        name="prep",
    )(step_raw, head_rates)


def conv_tile(buffer, raw, previous, taps):
    q = raw.shape[0]
    buffer[0:8, :] = previous
    buffer[8 : 8 + q, :] = raw.astype(F32)
    total = taps[0:1, :] * buffer[5 : 5 + q, :]
    for k in range(1, TAPS):
        total = total + taps[k : k + 1, :] * buffer[5 + k : 5 + k + q, :]
    return silu(total).astype(BF16), buffer[q : q + 8, :]


def pair(column_a, column_b, left):
    return jnp.where(left, column_a, column_b)


def states_kernel(
    group, per_group, pieces,
    x_ref, b_ref, c_ref, halo_x_ref, halo_b_ref, halo_c_ref, taps_x_ref, taps_b_ref, taps_c_ref,
    cum_ref, rel_ref, before_ref,
    xc_ref, bc_ref, cc_ref, local_ref, payload_ref,
    buffer, last_x, last_b, last_c, state,
):
    k = pl.program_id(0)
    q, width = x_ref.shape
    first = group * per_group

    @pl.when(k == 0)
    def _():
        last_x[...] = halo_x_ref[...].astype(F32)
        last_b[...] = halo_b_ref[...].astype(F32)
        last_c[...] = halo_c_ref[...].astype(F32)
        state[...] = jnp.zeros_like(state)

    b_now, last_b[...] = conv_tile(buffer.at[0], b_ref[...], last_b[...], taps_b_ref)
    bc_ref[...] = b_now
    cc_ref[...], last_c[...] = conv_tile(buffer.at[1], c_ref[...], last_c[...], taps_c_ref)
    b_t = jnp.transpose(b_now)
    left = lax.broadcasted_iota(jnp.int32, (q, LANES), 1) < HEAD_DIM
    left_row = lax.broadcasted_iota(jnp.int32, (1, LANES), 1) < HEAD_DIM
    final = cum_ref[q - 1 : q, :]
    tail_log = final - rel_ref[...]
    for p in range(width // LANES):
        cols = slice(p * LANES, (p + 1) * LANES)
        a, b = first + 2 * p, first + 2 * p + 1
        xc, last_x[:, cols] = conv_tile(
            buffer.at[p % 2], x_ref[:, cols], last_x[:, cols], taps_x_ref.at[:, cols]
        )
        xc_ref[:, cols] = xc
        weight = jnp.exp2(pair(tail_log[:, a : a + 1], tail_log[:, b : b + 1], left))
        tail = (weight * xc.astype(F32)).astype(BF16)
        decay = jnp.exp2(pair(final[:, a : a + 1], final[:, b : b + 1], left_row))
        held = state[:, cols]
        local_ref[0, :, cols] = held.astype(BF16)
        state[:, cols] = decay * held + dot(b_t, tail)

    @pl.when(k == pl.num_programs(0) - 1)
    def _():
        payload_ref[:, :width] = state[...].astype(BF16)
        blocks = before_ref.shape[0] - 1
        heads = before_ref.shape[1]
        decay = jnp.exp2(before_ref[blocks : blocks + 1, :])[:, first : first + per_group]
        high = decay.astype(BF16).astype(F32)
        low = decay - high
        place = lax.broadcasted_iota(jnp.int32, (STATE, per_group), 0) % (STATE // pieces)
        extra = jnp.where(place == 0, high, jnp.where(place == 1, low, 0.0))
        payload_ref[:, width:] = jnp.concatenate(
            [extra, jnp.zeros((STATE, LANES - per_group), F32)], 1
        ).astype(BF16)


def states(group, per_group, pieces, q, x, maps, halo, taps_x, taps_maps, cum, rel, before):
    rows, channels = x.shape
    heads = cum.shape[1]
    width = per_group * HEAD_DIM
    groups = channels // width
    blocks = rows // q
    halo_x, halo_maps = halo

    def at(shape, where):
        return pl.BlockSpec(shape, where)

    return pl.pallas_call(
        functools.partial(states_kernel, group, per_group, pieces),
        grid=(blocks,),
        in_specs=[
            at((q, width), lambda k: (k, group)),
            at((q, STATE), lambda k: (k, group)),
            at((q, STATE), lambda k: (k, groups + group)),
            at((8, width), lambda k: (0, group)),
            at((8, STATE), lambda k: (0, group)),
            at((8, STATE), lambda k: (0, groups + group)),
            at((TAPS, width), lambda k: (0, group)),
            at((TAPS, STATE), lambda k: (0, group)),
            at((TAPS, STATE), lambda k: (0, groups + group)),
            at((q, heads), lambda k: (k, 0)),
            at((q, heads), lambda k: (k, 0)),
            at((blocks + 1, heads), lambda k: (0, 0)),
        ],
        out_specs=[
            at((q, width), lambda k: (k, 0)),
            at((q, STATE), lambda k: (k, 0)),
            at((q, STATE), lambda k: (k, 0)),
            at((1, STATE, width), lambda k: (k, 0, 0)),
            at((STATE, width + LANES), lambda k: (0, 0)),
        ],
        out_shape=(
            jax.ShapeDtypeStruct((rows, width), BF16),
            jax.ShapeDtypeStruct((rows, STATE), BF16),
            jax.ShapeDtypeStruct((rows, STATE), BF16),
            jax.ShapeDtypeStruct((blocks, STATE, width), BF16),
            jax.ShapeDtypeStruct((STATE, width + LANES), BF16),
        ),
        scratch_shapes=[
            pltpu.VMEM((2, q + 8, LANES), F32),
            pltpu.VMEM((8, width), F32),
            pltpu.VMEM((8, STATE), F32),
            pltpu.VMEM((8, STATE), F32),
            pltpu.VMEM((STATE, width), F32),
        ],
        compiler_params=params(1),
        cost_estimate=cost(2 * rows * STATE * width, 8 * rows * width, 3 * rows * width),
        name="states",
    )(x, maps, maps, halo_x, halo_maps, halo_maps, taps_x, taps_maps, taps_maps, cum, rel, before)


def spread(width):
    row = lax.broadcasted_iota(jnp.int32, (LANES, width), 0)
    col = lax.broadcasted_iota(jnp.int32, (LANES, width), 1)
    return (col // HEAD_DIM == row).astype(BF16)


def scan_kernel(part_ref, out_ref):
    pieces, _, wide = part_ref.shape
    width = wide - LANES
    high = jnp.concatenate([part_ref[j, 0:1, width:] for j in range(pieces)], 0)
    low = jnp.concatenate([part_ref[j, 1:2, width:] for j in range(pieces)], 0)
    one_hot = spread(width)
    decay = dot(high, one_hot) + dot(low, one_hot)
    state = jnp.zeros(out_ref.shape[1:], F32)
    for j in range(pieces):
        out_ref[j] = state.astype(BF16)
        state = decay[j : j + 1, :] * state + part_ref[j, :, :width].astype(F32)


def scan_shards(part):
    pieces, depth, wide = part.shape
    return pl.pallas_call(
        scan_kernel,
        out_shape=jax.ShapeDtypeStruct((pieces, depth, wide - LANES), BF16),
        compiler_params=pltpu.CompilerParams(vmem_limit_bytes=VMEM_LIMIT),
        cost_estimate=cost(4 * pieces * depth * wide, 4 * pieces * depth * wide),
        name="scan_shards",
    )(part)


def outputs_kernel(
    group, per_group,
    where_ref, x_ref, b_ref, c_ref, cum_ref, rel_t_ref, before_ref, enter_ref, local_ref,
    gate_ref, gain_ref, skip_ref, *rest,
):
    out_ref, held = rest[-2:]
    q, width = x_ref.shape
    first = group * per_group
    block = where_ref[0] + pl.program_id(0)
    causal = lax.broadcasted_iota(jnp.int32, (q, q), 0) >= lax.broadcasted_iota(
        jnp.int32, (q, q), 1
    )
    left = lax.broadcasted_iota(jnp.int32, (q, LANES), 1) < HEAD_DIM
    left_row = lax.broadcasted_iota(jnp.int32, (1, LANES), 1) < HEAD_DIM
    c_now = c_ref[...]
    scores = dot(c_now, b_ref[...], ((1,), (1,)))
    before = before_ref[pl.ds(block, 1), :]
    cum = cum_ref[...]
    squares = jnp.zeros((q, LANES), F32)
    zero = jnp.zeros((q, LANES), BF16)
    for p in range(width // LANES):
        cols = slice(p * LANES, (p + 1) * LANES)
        weights = []
        logs = []
        for h in (first + 2 * p, first + 2 * p + 1):
            log_t = jnp.broadcast_to(cum[:, h : h + 1], (q, q))
            decay = jnp.exp2(log_t - rel_t_ref[0, h : h + 1, :])
            weights.append(jnp.where(causal, scores * decay, 0.0).astype(BF16))
            logs.append(cum[:, h : h + 1])
        a, b = first + 2 * p, first + 2 * p + 1
        x_now = x_ref[:, cols]
        stacked = jnp.concatenate([jnp.where(left, x_now, zero), jnp.where(left, zero, x_now)], 0)
        total = dot(jnp.concatenate(weights, 1), stacked)
        reach = jnp.exp2(pair(before[:, a : a + 1], before[:, b : b + 1], left_row))
        entering = reach * enter_ref[:, cols].astype(F32) + local_ref[0, :, cols].astype(F32)
        from_state = dot(c_now, entering.astype(BF16))
        total = total + jnp.exp2(pair(logs[0], logs[1], left)) * from_state
        total = total + skip_ref[:, cols] * x_now.astype(F32)
        total = total * silu(gate_ref[:, cols].astype(F32))
        held[:, cols] = total
        squares = squares + total * total
    mean = jnp.sum(squares, axis=1, keepdims=True) * (1.0 / width)
    inverse = lax.rsqrt(mean + EPSILON)
    for p in range(width // LANES):
        cols = slice(p * LANES, (p + 1) * LANES)
        out_ref[:, cols] = (held[:, cols] * inverse * gain_ref[:, cols]).astype(BF16)


def outputs(group, per_group, q, where, span, conved, cum, rel_t, before, enter, gate, gain, skip,
            token=None, target=None, column=None):
    xc, bc, cc, local = conved
    rows, width = xc.shape
    heads = cum.shape[1]
    blocks = rows // q
    scalars = jnp.stack([where] if column is None else [where, column])
    in_specs = [
        pl.BlockSpec((q, width), lambda i, s: (s[0] + i, 0)),
        pl.BlockSpec((q, STATE), lambda i, s: (s[0] + i, 0)),
        pl.BlockSpec((q, STATE), lambda i, s: (s[0] + i, 0)),
        pl.BlockSpec((q, heads), lambda i, s: (s[0] + i, 0)),
        pl.BlockSpec((1, heads, q), lambda i, s: (s[0] + i, 0, 0)),
        pl.BlockSpec((blocks + 1, heads), lambda i, s: (0, 0)),
        pl.BlockSpec((STATE, width), lambda i, s: (0, 0)),
        pl.BlockSpec((1, STATE, width), lambda i, s: (s[0] + i, 0, 0)),
        pl.BlockSpec((q, width), lambda i, s: (s[0] + i, group)),
        pl.BlockSpec((1, width), lambda i, s: (0, group)),
        pl.BlockSpec((1, width), lambda i, s: (0, group)),
    ]
    operands = [xc, bc, cc, cum, rel_t, before, enter, local, gate, gain, skip]
    if token is not None:
        in_specs.append(pl.BlockSpec(memory_space=pl.ANY))
        operands.append(token)
    aliases = {}
    if column is None:
        out_shape = jax.ShapeDtypeStruct((span, width), BF16)
        out_spec = pl.BlockSpec((q, width), lambda i, s: (i, 0))
    else:
        out_shape = jax.ShapeDtypeStruct(target, BF16) if isinstance(target, tuple) else (
            jax.ShapeDtypeStruct(target.shape, BF16)
        )
        out_spec = pl.BlockSpec((q, width), lambda i, s: (i, s[1]))
        if not isinstance(target, tuple):
            in_specs.append(pl.BlockSpec(memory_space=pl.ANY))
            operands.append(target)
            aliases = {len(operands): 0}
    return pl.pallas_call(
        functools.partial(outputs_kernel, group, per_group),
        grid_spec=pltpu.PrefetchScalarGridSpec(
            num_scalar_prefetch=1,
            grid=(span // q,),
            in_specs=in_specs,
            out_specs=out_spec,
            scratch_shapes=[pltpu.VMEM((q, width), F32)],
        ),
        out_shape=out_shape,
        input_output_aliases=aliases,
        compiler_params=params(1),
        cost_estimate=cost(span * width * (2 * STATE + 4 * q), 8 * span * width, span * width * 4),
        name="outputs",
    )(scalars, *operands)


def place_kernel(where_ref, block_ref, target_ref, out_ref):
    out_ref[...] = block_ref[...]


def place(target, block, column):
    rows, width = block.shape
    return pl.pallas_call(
        place_kernel,
        grid_spec=pltpu.PrefetchScalarGridSpec(
            num_scalar_prefetch=1,
            grid=(2,),
            in_specs=[
                pl.BlockSpec((rows // 2, width), lambda i, s: (i, 0)),
                pl.BlockSpec(memory_space=pl.ANY),
            ],
            out_specs=pl.BlockSpec((rows // 2, width), lambda i, s: (i, s[0])),
        ),
        out_shape=jax.ShapeDtypeStruct(target.shape, target.dtype),
        input_output_aliases={2: 0},
        compiler_params=params(1),
        cost_estimate=cost(0, 4 * rows * width),
        name="place",
    )(jnp.stack([column]), block, target)


def per_device(
    channels_in,
    state_maps,
    gate_in,
    step_raw,
    convolution_channel_taps,
    conv_maps,
    head_rates,
    skip_gain,
    norm_gain,
):
    rows, channels = channels_in.shape
    heads = step_raw.shape[1]
    map_width = state_maps.shape[2]
    groups = map_width // STATE
    per_group = heads // groups
    width = per_group * HEAD_DIM
    shards = lax.axis_size("ctx")
    peers = lax.axis_size("head")
    me = lax.axis_index("head")
    span = rows // peers
    q = LANES if span % LANES == 0 else HEAD_DIM

    maps = state_maps.reshape(rows, 2 * map_width)
    taps_maps = conv_maps.reshape(TAPS, 2 * map_width)
    ahead = [(i, i + 1) for i in range(shards - 1)]
    edge = jnp.concatenate([channels_in[rows - 8 :], maps[rows - 8 :]], 1)
    edge = lax.ppermute(edge, "ctx", ahead)
    halo = (edge[:, :channels], edge[:, channels:])

    cum, rel, rel_t, before = prep(step_raw, head_rates, q)
    skip = jnp.repeat(skip_gain, HEAD_DIM)[None, :]
    gain = norm_gain[None, :]

    conved, entering = [], []
    for group in range(groups):
        *local, payload = states(
            group, per_group, shards, q, channels_in, maps, halo,
            convolution_channel_taps, taps_maps, cum, rel, before,
        )
        conved.append(local)
        payload = payload.reshape(shards, STATE // shards, width + LANES)
        part = lax.all_to_all(payload, "ctx", 0, 0, tiled=True)
        enter = lax.all_to_all(scan_shards(part), "ctx", 0, 0, tiled=True)
        entering.append(enter.reshape(STATE, width))

    def block_of(group, far, **more):
        start = (me ^ far) * (span // q)
        return outputs(
            group, per_group, q, start, span, conved[group], cum, rel_t, before, entering[group],
            gate_in, gain, skip, **more,
        )

    arrived = []
    token = None
    order = [(far, group) for group in range(groups) for far in range(peers - 1, 1, -1)]
    order += [(1, group) for group in range(groups)]
    for far, group in order:
        token = block_of(group, far, token=token)
        pairs = [(i, i ^ far) for i in range(peers)]
        arrived.append((far, group, lax.ppermute(token, "head", pairs)))
    result = (span, channels * peers)
    for group in range(groups):
        result = block_of(group, 0, token=token, target=result, column=me * groups + group)
        token = None
    for far, group, block in arrived:
        result = place(result, block, (me ^ far) * groups + group)
    return result


def solution(mesh):
    return jax.shard_map(
        per_device,
        mesh=mesh,
        in_specs=(
            P("ctx", "head"),
            P("ctx", None, "head"),
            P("ctx", "head"),
            P("ctx", "head"),
            P(None, "head"),
            P(None, None, "head"),
            P(None, "head"),
            P("head"),
            P("head"),
        ),
        out_specs=P(("ctx", "head"), None),
        check_vma=False,
    )
```

```python
import functools
import math

import jax
import jax.numpy as jnp
import numpy as np
from jax import lax
from jax.experimental import pallas as pl
from jax.experimental.pallas import tpu as pltpu
from jax.sharding import PartitionSpec as P


HEAD_DIM = 64
STATE = 128
TAPS = 4
LANES = 128
SUB = 64
EPSILON = 1e-05
LOG2E = 1.0 / math.log(2.0)
HIGHEST = lax.Precision.HIGHEST
F32 = jnp.float32
BF16 = jnp.bfloat16
STATES_STEP = 3
SMALL_LIMIT = 8 * 1024 * 1024
VMEM_LIMIT = 60 * 1024 * 1024


def dot(a, b, dims=((1,), (0,)), precision=None):
    return lax.dot_general(a, b, (dims, ((), ())), precision=precision, preferred_element_type=F32)


def silu(v):
    half = 0.5 * v
    return half + half * jnp.tanh(half)


def params(n_dims):
    return pltpu.CompilerParams(
        dimension_semantics=("arbitrary",) * n_dims, vmem_limit_bytes=VMEM_LIMIT
    )


def cost(flops, bytes_accessed, transcendentals=0):
    return pl.CostEstimate(
        flops=int(flops), bytes_accessed=int(bytes_accessed), transcendentals=int(transcendentals)
    )


def prep_kernel(
    q, groups, step_ref, rates_ref, gains_ref, choose_ref,
    split_ref, spread_ref, rel_ref, before_ref, reach_ref, skip_ref, held,
):
    heads, rows = step_ref.shape
    upper = (
        lax.broadcasted_iota(jnp.int32, (q, q), 0) <= lax.broadcasted_iota(jnp.int32, (q, q), 1)
    ).astype(F32)
    lane = lax.broadcasted_iota(jnp.int32, (heads, LANES), 1)
    rates = jnp.transpose(jnp.concatenate([rates_ref[...], jnp.zeros((6, heads), F32)], 0))
    raw = step_ref[...] + rates[:, 0:1]
    step = jnp.maximum(raw, 0.0) + jnp.log1p(jnp.exp(-jnp.abs(raw)))
    rated = -LOG2E * jnp.exp(rates[:, 1:2]) * step
    shift = jnp.log(step) * LOG2E
    blocks = rows // q
    stacked = jnp.concatenate([rated[:, k * q : (k + 1) * q] for k in range(blocks)], 0)
    summed = dot(stacked, upper, precision=HIGHEST)
    before = jnp.zeros((heads, 1), F32)
    befores = jnp.zeros((heads, LANES), F32)
    for k in range(blocks):
        cum = summed[k * heads : (k + 1) * heads]
        final = cum[:, q - 1 : q]
        rel = cum - shift[:, k * q : (k + 1) * q]
        held[k] = rel
        even = held[k, pl.ds(0, heads // 2, stride=2), :]
        odd = held[k, pl.ds(1, heads // 2, stride=2), :]
        for j in range(q // SUB):
            part = slice(j * SUB, (j + 1) * SUB)
            rel_ref[k, j] = jnp.concatenate([even[:, part], odd[:, part]], 1)
        per_group = heads // groups
        cuts = [slice(g * per_group, (g + 1) * per_group) for g in range(groups)]
        parts = []
        for value in (jnp.exp2(final - rel), jnp.exp2(cum)):
            high = value.astype(BF16).astype(F32)
            parts += [high, value - high]
        parts = [part[cut] for cut in cuts for part in parts]
        rows_k = slice(k * q, (k + 1) * q)
        spread_ref[rows_k, :] = jnp.transpose(jnp.concatenate(parts, 0)).astype(BF16)
        high = cum.astype(BF16).astype(F32)
        middle = (cum - high).astype(BF16).astype(F32)
        parts = [high, middle, cum - high - middle, jnp.zeros_like(cum)]
        parts = [part[cut] for cut in cuts for part in parts]
        split_ref[rows_k, :] = jnp.transpose(jnp.concatenate(parts, 0)).astype(BF16)
        befores = jnp.where(lane == k, before, befores)
        before = before + final
    befores = jnp.where(lane == blocks, before, befores)
    before_ref[...] = jnp.transpose(befores)[: blocks + 1]
    by_head = jnp.concatenate([jnp.exp2(before_ref[...]), gains_ref[...]], 0)
    reach = dot(by_head, choose_ref[...], precision=HIGHEST)
    skip_ref[...] = reach[blocks + 1 :]
    for k in range(blocks + 1):
        reach_ref[k] = reach[k : k + 1]


def prep(step_raw, head_rates, skip_gain, q, groups):
    rows, heads = step_raw.shape
    blocks = rows // q
    choose = jnp.asarray(np.repeat(np.eye(heads, dtype=np.float32), HEAD_DIM, axis=1))
    return pl.pallas_call(
        functools.partial(prep_kernel, q, groups),
        out_shape=(
            jax.ShapeDtypeStruct((rows, 4 * heads), BF16),
            jax.ShapeDtypeStruct((rows, 4 * heads), BF16),
            jax.ShapeDtypeStruct((blocks, q // SUB, heads // 2, 2 * SUB), F32),
            jax.ShapeDtypeStruct((blocks + 1, heads), F32),
            jax.ShapeDtypeStruct((blocks + 1, 1, heads * HEAD_DIM), F32),
            jax.ShapeDtypeStruct((1, heads * HEAD_DIM), F32),
        ),
        scratch_shapes=[pltpu.VMEM((blocks, heads, q), F32)],
        compiler_params=pltpu.CompilerParams(vmem_limit_bytes=VMEM_LIMIT),
        cost_estimate=cost(rows * q * heads * 12, rows * heads * 16, rows * heads * 4),
        name="prep",
    )(step_raw.T, head_rates, skip_gain[None, :], choose)


def choice(per_group):
    one = np.repeat(np.eye(per_group, dtype=np.float32), HEAD_DIM, axis=1)
    return jnp.asarray(np.concatenate([one] * 3, 0), BF16)


def states_kernel(
    group, groups, pieces, q, starts, ends,
    x_ref, maps_ref, spread_ref, halo_ref, taps_x_ref, taps_m_ref, before_ref, choose_ref, *rest,
):
    xc_ref, mc_ref, local_ref, final_ref, carry_ref, buffer, last, state, weight, tail = rest[-10:]
    step = pl.program_id(0)
    width = x_ref.shape[1]
    heads = before_ref.shape[1]
    per_group = heads // groups
    channels = groups * width
    tiles = width // LANES
    sources = [(group * width + p * LANES) for p in range(tiles)]
    sources += [channels + group * STATE, channels + (groups + group) * STATE]

    @pl.when(step == 0)
    def _():
        if starts:
            for t, column in enumerate(sources):
                last[t] = halo_ref[:, column : column + LANES].astype(F32)
            state[...] = jnp.zeros_like(state)
        else:
            state[...] = rest[0][:STATE, :]
            for t in range(len(sources)):
                if t < tiles:
                    last[t] = rest[0][STATE : STATE + 8, t * LANES : (t + 1) * LANES]
                else:
                    place = (t - tiles) * LANES
                    last[t] = rest[0][STATE + 8 :, place : place + LANES]

    def conv(t, raw, taps):
        rows = buffer.at[t]
        rows[0:8, :] = last[t]
        rows[8 : 8 + q, :] = raw.astype(F32)
        half = taps[0:1, :] * rows[5 : 5 + q, :]
        for i in range(1, TAPS):
            half = half + taps[i : i + 1, :] * rows[5 + i : 5 + i + q, :]
        last[t] = rows[q : q + 8, :]
        return (half + half * jnp.tanh(half)).astype(BF16)

    def block(i):
        rows = pl.ds(pl.multiple_of(i * q, q), q)
        parts = group * 4 * per_group
        choose = choose_ref[: 2 * per_group, :]
        weight[...] = dot(spread_ref[rows, parts : parts + 2 * per_group], choose)
        for m in range(2):
            column = (m * groups + group) * STATE
            taps = 0.5 * taps_m_ref[:, m, group * STATE : (group + 1) * STATE]
            mc_ref[rows, m * STATE : (m + 1) * STATE] = conv(
                tiles + m, maps_ref[rows, column : column + STATE], taps
            )
        for p in range(tiles):
            cols = slice(p * LANES, (p + 1) * LANES)
            first = group * width + p * LANES
            xc = conv(p, x_ref[rows, cols], 0.5 * taps_x_ref[:, first : first + LANES])
            xc_ref[rows, cols] = xc
            tail[:, cols] = (weight[:, cols] * xc.astype(F32)).astype(BF16)
        tip = pl.ds(pl.multiple_of(i * q + q - 16, 16), 16)
        decay = dot(spread_ref[tip, parts + 2 * per_group : parts + 4 * per_group], choose)[15:16]
        held = state[...]
        local_ref[i] = held.astype(BF16)
        state[...] = decay * held + dot(jnp.transpose(mc_ref[rows, :STATE]), tail[...])

    pl.loop(0, x_ref.shape[0] // q)(block)

    @pl.when(step == pl.num_programs(0) - 1)
    def _():
        if not ends:
            carry_ref[:STATE, :] = state[...]
            for t in range(len(sources)):
                if t < tiles:
                    carry_ref[STATE : STATE + 8, t * LANES : (t + 1) * LANES] = last[t]
                else:
                    place = (t - tiles) * LANES
                    carry_ref[STATE + 8 :, place : place + LANES] = last[t]
            return
        payload_ref = final_ref
        payload_ref[:, :width] = state[...].astype(BF16)
        blocks = before_ref.shape[0] - 1
        first = group * per_group
        decay = jnp.exp2(before_ref[blocks : blocks + 1, :])[:, first : first + per_group]
        high = decay.astype(BF16).astype(F32)
        low = decay - high
        place = lax.broadcasted_iota(jnp.int32, (STATE, per_group), 0) % (STATE // pieces)
        extra = jnp.where(place == 0, high, jnp.where(place == 1, low, 0.0))
        payload_ref[:, width:] = jnp.concatenate(
            [extra, jnp.zeros((STATE, LANES - per_group), F32)], 1
        ).astype(BF16)


def whole(shape):
    return pl.BlockSpec(shape, lambda *_: (0,) * len(shape))


def states(group, groups, pieces, q, first, last, x, maps, halo, taps_x, taps_maps, spread_log,
           before, earlier=None):
    rows, channels = x.shape
    heads = before.shape[1]
    width = channels // groups
    blocks = rows // q
    starts, ends = first == 0, last == blocks
    step = math.gcd(STATES_STEP, math.gcd(first, last))
    skip = first // step

    in_specs = [
        pl.BlockSpec((step * q, width), lambda k: (skip + k, group)),
        pl.BlockSpec((step * q, maps.shape[1]), lambda k: (skip + k, 0)),
        pl.BlockSpec((step * q, 4 * heads), lambda k: (skip + k, 0)),
    ]
    operands = [
        x, maps, spread_log, halo, taps_x, taps_maps, before,
        choice(heads // groups),
    ]
    in_specs += [whole(a.shape) for a in operands[3:]]
    aliases = {}
    if earlier is not None:
        in_specs += [whole(earlier[4].shape)] + [pl.BlockSpec(memory_space=pl.ANY)] * 3
        operands += [earlier[4], *earlier[:3]]
        aliases = {len(operands) - 3 + i: i for i in range(3)}
    final = (STATE, width + LANES) if ends else (8, LANES)
    carry = (8, LANES) if ends else (STATE + 16, width)
    return pl.pallas_call(
        functools.partial(states_kernel, group, groups, pieces, q, starts, ends),
        grid=((last - first) // step,),
        in_specs=in_specs,
        out_specs=[
            pl.BlockSpec((step * q, width), lambda k: (skip + k, 0)),
            pl.BlockSpec((step * q, 2 * STATE), lambda k: (skip + k, 0)),
            pl.BlockSpec((step, STATE, width), lambda k: (skip + k, 0, 0)),
            pl.BlockSpec(final, lambda k: (0, 0)),
            pl.BlockSpec(carry, lambda k: (0, 0)),
        ],
        out_shape=(
            jax.ShapeDtypeStruct((rows, width), BF16),
            jax.ShapeDtypeStruct((rows, 2 * STATE), BF16),
            jax.ShapeDtypeStruct((blocks, STATE, width), BF16),
            jax.ShapeDtypeStruct(final, BF16),
            jax.ShapeDtypeStruct(carry, F32),
        ),
        input_output_aliases=aliases,
        scratch_shapes=[
            pltpu.VMEM((2 + width // LANES, q + 8, LANES), F32),
            pltpu.VMEM((2 + width // LANES, 8, LANES), F32),
            pltpu.VMEM((STATE, width), F32),
            pltpu.VMEM((q, width), F32),
            pltpu.VMEM((q, width), BF16),
        ],
        compiler_params=params(1),
        cost_estimate=cost(
            2 * (last - first) * q * STATE * width,
            8 * (last - first) * q * width,
            3 * (last - first) * q * width,
        ),
        name="states",
    )(*operands)


def spread(width):
    row = lax.broadcasted_iota(jnp.int32, (LANES, width), 0)
    col = lax.broadcasted_iota(jnp.int32, (LANES, width), 1)
    return (col // HEAD_DIM == row).astype(BF16)


def scan_kernel(part_ref, out_ref):
    pieces, _, wide = part_ref.shape
    width = wide - LANES
    high = jnp.concatenate([part_ref[j, 0:1, width:] for j in range(pieces)], 0)
    low = jnp.concatenate([part_ref[j, 1:2, width:] for j in range(pieces)], 0)
    one_hot = spread(width)
    decay = dot(high, one_hot) + dot(low, one_hot)
    state = jnp.zeros(out_ref.shape[1:], F32)
    for j in range(pieces):
        out_ref[j] = state.astype(BF16)
        state = decay[j : j + 1, :] * state + part_ref[j, :, :width].astype(F32)


def scan_shards(part):
    pieces, depth, wide = part.shape
    return pl.pallas_call(
        scan_kernel,
        out_shape=jax.ShapeDtypeStruct((pieces, depth, wide - LANES), BF16),
        compiler_params=pltpu.CompilerParams(vmem_limit_bytes=SMALL_LIMIT),
        cost_estimate=cost(4 * pieces * depth * wide, 4 * pieces * depth * wide),
        name="scan_shards",
    )(part)


def outputs_kernel(
    group, near,
    where_ref, x_ref, maps_ref, gate_ref, split_ref, rel_ref, spread_ref, reach_ref, local_ref,
    enter_ref, choose_ref, gain_ref, skip_ref, *rest,
):
    held, logs = rest[-2:]
    q, width = x_ref.shape
    tiles = width // LANES
    subs = q // SUB
    row = lax.broadcasted_iota(jnp.int32, (SUB, LANES), 0)
    lane = lax.broadcasted_iota(jnp.int32, (SUB, LANES), 1)
    causal = row >= lane % SUB
    left = lane < HEAD_DIM
    zero = jnp.zeros((SUB, LANES), BF16)
    c_now = maps_ref[:, STATE:]
    scores = []
    for j in range(subs):
        b_now = maps_ref[j * SUB : (j + 1) * SUB, :STATE]
        twice = jnp.concatenate([b_now, b_now], 0)
        scores.append(dot(c_now[j * SUB :], twice, ((1,), (1,))))
    wide = min(width, 2 * LANES)
    per_group = width // HEAD_DIM
    parts = group * 4 * per_group
    grown = spread_ref[:, parts + 2 * per_group : parts + 4 * per_group]
    split = split_ref[:, parts : parts + 3 * per_group]
    for first in range(0, width, wide):
        cols = slice(first, first + wide)
        held[:, cols] = reach_ref[0, :, cols] * dot(c_now, enter_ref[:, cols])
        held[:, cols] = held[:, cols] + dot(c_now, local_ref[0, :, cols])
        held[:, cols] = held[:, cols] * dot(grown, choose_ref[: 2 * per_group, cols])
        logs[:, cols] = dot(split, choose_ref[:, cols])
    squares = [jnp.zeros((SUB, LANES), F32) for _ in range(subs)]
    for p in range(tiles):
        cols = slice(p * LANES, (p + 1) * LANES)
        stacked = []
        for i in range(subs):
            rows = slice(i * SUB, (i + 1) * SUB)
            x_now = x_ref[rows, cols]
            stacked += [jnp.where(left, x_now, zero), jnp.where(left, zero, x_now)]
            weights = []
            for j in range(i + 1):
                decay = jnp.exp2(logs[rows, cols] - rel_ref[0, j, group * tiles + p, :][None, :])
                weight = scores[j][(i - j) * SUB : (i - j + 1) * SUB] * decay
                weights.append((jnp.where(causal, weight, 0.0) if i == j else weight).astype(BF16))
            total = held[rows, cols] + skip_ref[:, cols] * x_now.astype(F32)
            total = total + dot(jnp.concatenate(weights, 1), jnp.concatenate(stacked, 0))
            total = total * silu(gate_ref[rows, cols].astype(F32))
            held[rows, cols] = total
            squares[i] = squares[i] + total * total

    def store(out_ref):
        for i in range(subs):
            rows = slice(i * SUB, (i + 1) * SUB)
            mean = jnp.sum(squares[i], axis=1, keepdims=True) * (1.0 / width)
            inverse = lax.rsqrt(mean + EPSILON)
            for p in range(tiles):
                cols = slice(p * LANES, (p + 1) * LANES)
                out_ref[rows, cols] = (held[rows, cols] * inverse * gain_ref[:, cols]).astype(BF16)

    if near:
        pl.when(pl.program_id(0) < near)(lambda: store(rest[-4]))
        pl.when(pl.program_id(0) >= near)(lambda: store(rest[-3]))
    else:
        store(rest[-3])


def outputs(group, groups, q, far, first, count, span, me, conved, logs, enter, gate, gain,
            token=None, target=None):
    xc, mc, local = conved
    split, spread_log, rel, before, reach, skip = logs
    _, width = xc.shape
    heads = before.shape[1]
    blocks = span // q
    home = target is not None and far > 0
    own = target is not None and far == 0

    def at(i, s):
        if home:
            return (s[0] ^ jnp.where(i < blocks, 1, 0)) * blocks + lax.rem(i, blocks)
        return (s[0] ^ far) * blocks + first + i

    in_specs = [
        pl.BlockSpec((q, width), lambda i, s: (at(i, s), 0)),
        pl.BlockSpec((q, 2 * STATE), lambda i, s: (at(i, s), 0)),
        pl.BlockSpec((q, width), lambda i, s: (at(i, s), group)),
        pl.BlockSpec((q, 4 * heads), lambda i, s: (at(i, s), 0)),
        pl.BlockSpec((1, q // SUB, heads // 2, LANES), lambda i, s: (at(i, s), 0, 0, 0)),
        pl.BlockSpec((q, 4 * heads), lambda i, s: (at(i, s), 0)),
        pl.BlockSpec((1, 1, width), lambda i, s: (at(i, s), 0, group)),
        pl.BlockSpec((1, STATE, width), lambda i, s: (at(i, s), 0, 0)),
        whole((STATE, width)),
        whole((3 * width // HEAD_DIM, width)),
        pl.BlockSpec((1, width), lambda i, s: (0, group)),
        pl.BlockSpec((1, width), lambda i, s: (0, group)),
    ]
    operands = [
        xc, mc, gate, split, rel, spread_log, reach, local,
        enter, choice(heads // groups), gain, skip,
    ]
    if token is not None:
        in_specs.append(pl.BlockSpec(memory_space=pl.ANY))
        operands.append(token)
    aliases = {}
    if home or own:
        start = blocks if home else 0
        count = start + blocks
        out_shape, out_specs = [], []
        if home:
            out_shape.append(jax.ShapeDtypeStruct((span, width), BF16))
            out_specs.append(pl.BlockSpec((q, width), lambda i, s: (jnp.minimum(i, blocks - 1), 0)))
        out_specs.append(
            pl.BlockSpec((q, width), lambda i, s: (jnp.maximum(i - start, 0), s[0] * groups + group))
        )
        if isinstance(target, tuple):
            out_shape.append(jax.ShapeDtypeStruct(target, BF16))
        else:
            out_shape.append(jax.ShapeDtypeStruct(target.shape, BF16))
            in_specs.append(pl.BlockSpec(memory_space=pl.ANY))
            operands.append(target)
            aliases = {len(operands): len(out_shape) - 1}
    else:
        out_shape = jax.ShapeDtypeStruct((count * q, width), BF16)
        out_specs = pl.BlockSpec((q, width), lambda i, s: (i, 0))
    return pl.pallas_call(
        functools.partial(outputs_kernel, group, blocks if home else 0),
        grid_spec=pltpu.PrefetchScalarGridSpec(
            num_scalar_prefetch=1,
            grid=(count,),
            in_specs=in_specs,
            out_specs=out_specs,
            scratch_shapes=[pltpu.VMEM((q, width), F32)] * 2,
        ),
        out_shape=out_shape,
        input_output_aliases=aliases,
        compiler_params=params(1),
        cost_estimate=cost(
            count * q * width * (2 * STATE + 4 * q), 8 * count * q * width, count * q * width * 4
        ),
        name="outputs",
    )(me, *operands)


def place_kernel(places, width, me_ref, *refs):
    count = len(places)
    out_ref, held, taken, put = refs[count + 1 :]
    copies = []
    at = 0
    for i, (far, group, groups, first, rows) in enumerate(places):
        slot = held.at[pl.ds(at, rows), :]
        column = pl.multiple_of(((me_ref[0] ^ far) * groups + group) * width, width)
        into = out_ref.at[pl.ds(first, rows), pl.ds(column, width)]
        copies.append(
            (
                pltpu.make_async_copy(refs[i], slot, taken.at[i]),
                pltpu.make_async_copy(slot, into, put.at[i]),
            )
        )
        at += rows
    for take, _ in copies:
        take.start()
    for take, give in copies:
        take.wait()
        give.start()
    for _, give in copies:
        give.wait()


def place(target, blocks, places, me):
    width = blocks[0].shape[1]
    total = sum(block.shape[0] for block in blocks)
    count = len(blocks)
    return pl.pallas_call(
        functools.partial(place_kernel, places, width),
        in_specs=[pl.BlockSpec(memory_space=pltpu.SMEM)]
        + [pl.BlockSpec(memory_space=pl.ANY)] * (count + 1),
        out_specs=pl.BlockSpec(memory_space=pl.ANY),
        out_shape=jax.ShapeDtypeStruct(target.shape, target.dtype),
        scratch_shapes=[
            pltpu.VMEM((total, width), BF16),
            pltpu.SemaphoreType.DMA((count,)),
            pltpu.SemaphoreType.DMA((count,)),
        ],
        input_output_aliases={count + 1: 0},
        compiler_params=pltpu.CompilerParams(vmem_limit_bytes=SMALL_LIMIT),
        cost_estimate=cost(0, 4 * total * width),
        name="place",
    )(me, *blocks, target)


def per_device(
    channels_in,
    state_maps,
    gate_in,
    step_raw,
    convolution_channel_taps,
    conv_maps,
    head_rates,
    skip_gain,
    norm_gain,
):
    rows, channels = channels_in.shape
    heads = step_raw.shape[1]
    map_width = state_maps.shape[2]
    groups = map_width // STATE
    width = heads // groups * HEAD_DIM
    shards = lax.axis_size("ctx")
    peers = lax.axis_size("head")
    me = lax.axis_index("head").reshape(1)
    span = rows // peers
    q = LANES if span % LANES == 0 else HEAD_DIM

    maps = state_maps.reshape(rows, 2 * map_width)
    ahead = [(i, i + 1) for i in range(shards - 1)]
    edge = jnp.concatenate([channels_in[rows - 8 :], maps[rows - 8 :]], 1)
    halo = lax.ppermute(edge, "ctx", ahead)

    logs = prep(step_raw, head_rates, skip_gain, q, groups)
    gain = norm_gain[None, :]

    def shard_states(group):
        blocks = rows // q
        cuts = [0, blocks] if group == 0 else [0, blocks // 2, blocks]
        done = None
        for first, last in zip(cuts[:-1], cuts[1:]):
            done = states(
                group, groups, shards, q, first, last, channels_in, maps, halo,
                convolution_channel_taps, conv_maps, logs[1], logs[3], done,
            )
        return done[:3], done[3].reshape(shards, STATE // shards, width + LANES)

    def exchange(payload):
        return lax.all_to_all(payload, "ctx", 0, 0, tiled=True)

    def block_of(group, far, first, count, **more):
        return outputs(
            group, groups, q, far, first, count, span, me, conved[group], logs, entering[group],
            gate_in, gain, **more,
        )

    def send(block, far):
        return lax.ppermute(block, "head", [(i, i ^ far) for i in range(peers)])

    conved, payloads = zip(*[shard_states(group) for group in range(groups)])
    entering, arrived, tokens = [], [], []
    blocks = span // q
    result = (span, channels * peers)
    for group in range(groups):
        payload = payloads[group]
        if group > 0:
            payload, _ = lax.optimization_barrier((payload, tokens[1]))
        part = exchange(payload)
        part = scan_shards(part)
        entering.append(exchange(part).reshape(STATE, width))
        for far in range(peers - 1, 1, -1):
            for first, last in sends(group, groups, far, peers, blocks):
                block = block_of(
                    group, far, first, last - first, token=tokens[-1] if tokens else None
                )
                tokens.append(block)
                arrived.append((send(block, far), (far, group, groups, first * q, (last - first) * q)))
        if group < groups - 1:
            home = block_of(group, 1, 0, blocks, token=tokens[-1])
            arrived.append((send(home, 1), (1, group, groups, 0, span)))
    for group in range(groups):
        if group < groups - 1:
            (result,) = block_of(group, 0, 0, blocks, token=tokens[-1], target=result)
        else:
            home, result = block_of(group, 1, 0, blocks, token=tokens[-1], target=result)
    arrived.append((send(home, 1), (1, groups - 1, groups, 0, span)))
    arrived.sort(key=lambda a: (a[1][1] == groups - 1 and a[1][0] > 1))
    late = sum(a[1][1] == groups - 1 and a[1][0] > 1 for a in arrived)
    cuts = [0, len(arrived) - late, len(arrived) - 1, len(arrived)]
    for low, high in zip(cuts[:-1], cuts[1:]):
        if high > low:
            part = arrived[low:high]
            result = place(result, [a[0] for a in part], [a[1] for a in part], me)
    return result


def sends(group, groups, far, peers, blocks):
    if blocks > 1 and far == peers - 1:
        return [(0, 1), (1, blocks)]
    if blocks > 1 and group == groups - 1 and far == 2:
        return [(0, blocks - 1), (blocks - 1, blocks)]
    return [(0, blocks)]


def solution(mesh):
    return jax.shard_map(
        per_device,
        mesh=mesh,
        in_specs=(
            P("ctx", "head"),
            P("ctx", None, "head"),
            P("ctx", "head"),
            P("ctx", "head"),
            P(None, "head"),
            P(None, None, "head"),
            P(None, "head"),
            P("head"),
            P("head"),
        ),
        out_specs=P(("ctx", "head"), None),
        check_vma=False,
    )
```

```python
import functools
import math

import jax
import jax.numpy as jnp
import numpy as np
from jax import lax
from jax.experimental import pallas as pl
from jax.experimental.pallas import tpu as pltpu
from jax.sharding import PartitionSpec as P


HEAD_DIM = 64
STATE = 128
TAPS = 4
LANES = 128
SUB = 64
EPSILON = 1e-05
LOG2E = 1.0 / math.log(2.0)
HIGHEST = lax.Precision.HIGHEST
F32 = jnp.float32
BF16 = jnp.bfloat16
STATES_STEP = 3
SMALL_LIMIT = 8 * 1024 * 1024
VMEM_LIMIT = 60 * 1024 * 1024


def dot(a, b, dims=((1,), (0,)), precision=None):
    return lax.dot_general(a, b, (dims, ((), ())), precision=precision, preferred_element_type=F32)


def silu(v):
    half = 0.5 * v
    return half + half * jnp.tanh(half)


def params(n_dims):
    return pltpu.CompilerParams(
        dimension_semantics=("arbitrary",) * n_dims, vmem_limit_bytes=VMEM_LIMIT
    )


def cost(flops, bytes_accessed, transcendentals=0):
    return pl.CostEstimate(
        flops=int(flops), bytes_accessed=int(bytes_accessed), transcendentals=int(transcendentals)
    )


def prep_kernel(
    q, groups, step_ref, rates_ref, gains_ref, choose_ref,
    split_ref, spread_ref, rel_ref, before_ref, reach_ref, skip_ref, held,
):
    heads, rows = step_ref.shape
    upper = (
        lax.broadcasted_iota(jnp.int32, (q, q), 0) <= lax.broadcasted_iota(jnp.int32, (q, q), 1)
    ).astype(F32)
    lane = lax.broadcasted_iota(jnp.int32, (heads, LANES), 1)
    rates = jnp.transpose(jnp.concatenate([rates_ref[...], jnp.zeros((6, heads), F32)], 0))
    raw = step_ref[...] + rates[:, 0:1]
    step = jnp.maximum(raw, 0.0) + jnp.log1p(jnp.exp(-jnp.abs(raw)))
    rated = -LOG2E * jnp.exp(rates[:, 1:2]) * step
    shift = jnp.log(step) * LOG2E
    blocks = rows // q
    stacked = jnp.concatenate([rated[:, k * q : (k + 1) * q] for k in range(blocks)], 0)
    summed = dot(stacked, upper, precision=HIGHEST)
    before = jnp.zeros((heads, 1), F32)
    befores = jnp.zeros((heads, LANES), F32)
    for k in range(blocks):
        cum = summed[k * heads : (k + 1) * heads]
        final = cum[:, q - 1 : q]
        rel = cum - shift[:, k * q : (k + 1) * q]
        held[k, :heads] = rel
        even = held[k, pl.ds(0, heads // 2, stride=2), :]
        odd = held[k, pl.ds(1, heads // 2, stride=2), :]
        for j in range(q // SUB):
            part = slice(j * SUB, (j + 1) * SUB)
            rel_ref[k, j] = jnp.concatenate([even[:, part], odd[:, part]], 1)
        per_group = heads // groups
        cuts = [slice(g * per_group, (g + 1) * per_group) for g in range(groups)]
        parts = []
        for value in (jnp.exp2(final - rel), jnp.exp2(cum)):
            high = value.astype(BF16).astype(F32)
            parts += [high, value - high]
        parts = [part[cut] for cut in cuts for part in parts]
        rows_k = slice(k * q, (k + 1) * q)
        spread_ref[rows_k, :] = jnp.transpose(jnp.concatenate(parts, 0)).astype(BF16)
        high = cum.astype(BF16).astype(F32)
        middle = (cum - high).astype(BF16).astype(F32)
        parts = [high, middle, cum - high - middle, jnp.zeros_like(cum)]
        parts = [part[cut] for cut in cuts for part in parts]
        split_ref[rows_k, :] = jnp.transpose(jnp.concatenate(parts, 0)).astype(BF16)
        befores = jnp.where(lane == k, before, befores)
        before = before + final
    befores = jnp.where(lane == blocks, before, befores)
    before_ref[...] = jnp.transpose(befores)[: blocks + 1]
    by_head = jnp.concatenate([jnp.exp2(before_ref[...]), gains_ref[...]], 0)
    reach = dot(by_head, choose_ref[...], precision=HIGHEST)
    skip_ref[...] = reach[blocks + 1 :]
    for k in range(blocks + 1):
        reach_ref[k] = reach[k : k + 1]


def prep(step_raw, head_rates, skip_gain, q, groups):
    rows, heads = step_raw.shape
    blocks = rows // q
    choose = jnp.asarray(np.repeat(np.eye(heads, dtype=np.float32), HEAD_DIM, axis=1))
    return pl.pallas_call(
        functools.partial(prep_kernel, q, groups),
        out_shape=(
            jax.ShapeDtypeStruct((rows, 4 * heads), BF16),
            jax.ShapeDtypeStruct((rows, 4 * heads), BF16),
            jax.ShapeDtypeStruct((blocks, q // SUB, heads // 2, 2 * SUB), F32),
            jax.ShapeDtypeStruct((blocks + 1, heads), F32),
            jax.ShapeDtypeStruct((blocks + 1, 1, heads * HEAD_DIM), F32),
            jax.ShapeDtypeStruct((1, heads * HEAD_DIM), F32),
        ),
        scratch_shapes=[pltpu.VMEM((blocks, heads + 8, q), F32)],
        compiler_params=pltpu.CompilerParams(vmem_limit_bytes=VMEM_LIMIT),
        cost_estimate=cost(rows * q * heads * 12, rows * heads * 16, rows * heads * 4),
        name="prep",
    )(step_raw.T, head_rates, skip_gain[None, :], choose)


def choice(per_group):
    one = np.repeat(np.eye(per_group, dtype=np.float32), HEAD_DIM, axis=1)
    return jnp.asarray(np.concatenate([one] * 3, 0), BF16)


def states_kernel(
    group, groups, pieces, q, starts, ends,
    x_ref, maps_ref, spread_ref, halo_ref, taps_x_ref, taps_m_ref, before_ref, choose_ref, *rest,
):
    xc_ref, mc_ref, local_ref, final_ref, carry_ref, buffer, last, state, weight, tail = rest[-10:]
    step = pl.program_id(0)
    width = x_ref.shape[1]
    heads = before_ref.shape[1]
    per_group = heads // groups
    channels = groups * width
    tiles = width // LANES
    sources = [(group * width + p * LANES) for p in range(tiles)]
    sources += [channels + group * STATE, channels + (groups + group) * STATE]

    @pl.when(step == 0)
    def _():
        if starts:
            for t, column in enumerate(sources):
                last[t] = halo_ref[:, column : column + LANES].astype(F32)
            state[...] = jnp.zeros_like(state)
        else:
            state[...] = rest[0][:STATE, :]
            for t in range(len(sources)):
                if t < tiles:
                    last[t] = rest[0][STATE : STATE + 8, t * LANES : (t + 1) * LANES]
                else:
                    place = (t - tiles) * LANES
                    last[t] = rest[0][STATE + 8 :, place : place + LANES]

    def conv(t, raw, taps):
        rows = buffer.at[t]
        rows[0:8, :] = last[t]
        rows[8 : 8 + q, :] = raw.astype(F32)
        half = taps[0:1, :] * rows[5 : 5 + q, :]
        for i in range(1, TAPS):
            half = half + taps[i : i + 1, :] * rows[5 + i : 5 + i + q, :]
        last[t] = rows[q : q + 8, :]
        return (half + half * jnp.tanh(half)).astype(BF16)

    def block(i):
        rows = pl.ds(pl.multiple_of(i * q, q), q)
        parts = group * 4 * per_group
        choose = choose_ref[: 2 * per_group, :]
        weight[...] = dot(spread_ref[rows, parts : parts + 2 * per_group], choose)
        for m in range(2):
            column = (m * groups + group) * STATE
            taps = 0.5 * taps_m_ref[:, m, group * STATE : (group + 1) * STATE]
            mc_ref[rows, m * STATE : (m + 1) * STATE] = conv(
                tiles + m, maps_ref[rows, column : column + STATE], taps
            )
        for p in range(tiles):
            cols = slice(p * LANES, (p + 1) * LANES)
            first = group * width + p * LANES
            xc = conv(p, x_ref[rows, cols], 0.5 * taps_x_ref[:, first : first + LANES])
            xc_ref[rows, cols] = xc
            tail[:, cols] = (weight[:, cols] * xc.astype(F32)).astype(BF16)
        tip = pl.ds(pl.multiple_of(i * q + q - 16, 16), 16)
        decay = dot(spread_ref[tip, parts + 2 * per_group : parts + 4 * per_group], choose)[15:16]
        held = state[...]
        local_ref[i] = held.astype(BF16)
        state[...] = decay * held + dot(jnp.transpose(mc_ref[rows, :STATE]), tail[...])

    pl.loop(0, x_ref.shape[0] // q)(block)

    @pl.when(step == pl.num_programs(0) - 1)
    def _():
        if not ends:
            carry_ref[:STATE, :] = state[...]
            for t in range(len(sources)):
                if t < tiles:
                    carry_ref[STATE : STATE + 8, t * LANES : (t + 1) * LANES] = last[t]
                else:
                    place = (t - tiles) * LANES
                    carry_ref[STATE + 8 :, place : place + LANES] = last[t]
            return
        payload_ref = final_ref
        payload_ref[:, :width] = state[...].astype(BF16)
        blocks = before_ref.shape[0] - 1
        first = group * per_group
        decay = jnp.exp2(before_ref[blocks : blocks + 1, :])[:, first : first + per_group]
        high = decay.astype(BF16).astype(F32)
        low = decay - high
        place = lax.broadcasted_iota(jnp.int32, (STATE, per_group), 0) % (STATE // pieces)
        extra = jnp.where(place == 0, high, jnp.where(place == 1, low, 0.0))
        payload_ref[:, width:] = jnp.concatenate(
            [extra, jnp.zeros((STATE, LANES - per_group), F32)], 1
        ).astype(BF16)


def whole(shape):
    return pl.BlockSpec(shape, lambda *_: (0,) * len(shape))


def states(group, groups, pieces, q, first, last, x, maps, halo, taps_x, taps_maps, spread_log,
           before, earlier=None):
    rows, channels = x.shape
    heads = before.shape[1]
    width = channels // groups
    blocks = rows // q
    starts, ends = first == 0, last == blocks
    step = math.gcd(STATES_STEP, math.gcd(first, last))
    skip = first // step

    in_specs = [
        pl.BlockSpec((step * q, width), lambda k: (skip + k, group)),
        pl.BlockSpec((step * q, maps.shape[1]), lambda k: (skip + k, 0)),
        pl.BlockSpec((step * q, 4 * heads), lambda k: (skip + k, 0)),
    ]
    operands = [
        x, maps, spread_log, halo, taps_x, taps_maps, before,
        choice(heads // groups),
    ]
    in_specs += [whole(a.shape) for a in operands[3:]]
    aliases = {}
    if earlier is not None:
        in_specs += [whole(earlier[4].shape)] + [pl.BlockSpec(memory_space=pl.ANY)] * 3
        operands += [earlier[4], *earlier[:3]]
        aliases = {len(operands) - 3 + i: i for i in range(3)}
    final = (STATE, width + LANES) if ends else (8, LANES)
    carry = (8, LANES) if ends else (STATE + 16, width)
    return pl.pallas_call(
        functools.partial(states_kernel, group, groups, pieces, q, starts, ends),
        grid=((last - first) // step,),
        in_specs=in_specs,
        out_specs=[
            pl.BlockSpec((step * q, width), lambda k: (skip + k, 0)),
            pl.BlockSpec((step * q, 2 * STATE), lambda k: (skip + k, 0)),
            pl.BlockSpec((step, STATE, width), lambda k: (skip + k, 0, 0)),
            pl.BlockSpec(final, lambda k: (0, 0)),
            pl.BlockSpec(carry, lambda k: (0, 0)),
        ],
        out_shape=(
            jax.ShapeDtypeStruct((rows, width), BF16),
            jax.ShapeDtypeStruct((rows, 2 * STATE), BF16),
            jax.ShapeDtypeStruct((blocks, STATE, width), BF16),
            jax.ShapeDtypeStruct(final, BF16),
            jax.ShapeDtypeStruct(carry, F32),
        ),
        input_output_aliases=aliases,
        scratch_shapes=[
            pltpu.VMEM((2 + width // LANES, q + 8, LANES), F32),
            pltpu.VMEM((2 + width // LANES, 8, LANES), F32),
            pltpu.VMEM((STATE, width), F32),
            pltpu.VMEM((q, width), F32),
            pltpu.VMEM((q, width), BF16),
        ],
        compiler_params=params(1),
        cost_estimate=cost(
            2 * (last - first) * q * STATE * width,
            8 * (last - first) * q * width,
            3 * (last - first) * q * width,
        ),
        name="states",
    )(*operands)


def spread(width):
    row = lax.broadcasted_iota(jnp.int32, (LANES, width), 0)
    col = lax.broadcasted_iota(jnp.int32, (LANES, width), 1)
    return (col // HEAD_DIM == row).astype(BF16)


def scan_kernel(part_ref, out_ref):
    pieces, _, wide = part_ref.shape
    width = wide - LANES
    high = jnp.concatenate([part_ref[j, 0:1, width:] for j in range(pieces)], 0)
    low = jnp.concatenate([part_ref[j, 1:2, width:] for j in range(pieces)], 0)
    one_hot = spread(width)
    decay = dot(high, one_hot) + dot(low, one_hot)
    state = jnp.zeros(out_ref.shape[1:], F32)
    for j in range(pieces):
        out_ref[j] = state.astype(BF16)
        state = decay[j : j + 1, :] * state + part_ref[j, :, :width].astype(F32)


def scan_shards(part):
    pieces, depth, wide = part.shape
    return pl.pallas_call(
        scan_kernel,
        out_shape=jax.ShapeDtypeStruct((pieces, depth, wide - LANES), BF16),
        compiler_params=pltpu.CompilerParams(vmem_limit_bytes=SMALL_LIMIT),
        cost_estimate=cost(4 * pieces * depth * wide, 4 * pieces * depth * wide),
        name="scan_shards",
    )(part)


def outputs_kernel(
    group, near,
    where_ref, x_ref, maps_ref, gate_ref, split_ref, rel_ref, spread_ref, reach_ref, local_ref,
    enter_ref, choose_ref, gain_ref, skip_ref, *rest,
):
    held, logs = rest[-2:]
    q, width = x_ref.shape
    tiles = width // LANES
    subs = q // SUB
    row = lax.broadcasted_iota(jnp.int32, (SUB, LANES), 0)
    lane = lax.broadcasted_iota(jnp.int32, (SUB, LANES), 1)
    causal = row >= lane % SUB
    left = lane < HEAD_DIM
    zero = jnp.zeros((SUB, LANES), BF16)
    c_now = maps_ref[:, STATE:]
    scores = []
    for j in range(subs):
        b_now = maps_ref[j * SUB : (j + 1) * SUB, :STATE]
        twice = jnp.concatenate([b_now, b_now], 0)
        scores.append(dot(c_now[j * SUB :], twice, ((1,), (1,))))
    wide = min(width, 2 * LANES)
    per_group = width // HEAD_DIM
    parts = group * 4 * per_group
    grown = spread_ref[:, parts + 2 * per_group : parts + 4 * per_group]
    split = split_ref[:, parts : parts + 3 * per_group]
    for first in range(0, width, wide):
        cols = slice(first, first + wide)
        held[:, cols] = reach_ref[0, :, cols] * dot(c_now, enter_ref[:, cols])
        held[:, cols] = held[:, cols] + dot(c_now, local_ref[0, :, cols])
        held[:, cols] = held[:, cols] * dot(grown, choose_ref[: 2 * per_group, cols])
        logs[:, cols] = dot(split, choose_ref[:, cols])
    squares = [jnp.zeros((SUB, LANES), F32) for _ in range(subs)]
    for p in range(tiles):
        cols = slice(p * LANES, (p + 1) * LANES)
        stacked = []
        for i in range(subs):
            rows = slice(i * SUB, (i + 1) * SUB)
            x_now = x_ref[rows, cols]
            stacked += [jnp.where(left, x_now, zero), jnp.where(left, zero, x_now)]
            weights = []
            for j in range(i + 1):
                decay = jnp.exp2(logs[rows, cols] - rel_ref[0, j, group * tiles + p, :][None, :])
                weight = scores[j][(i - j) * SUB : (i - j + 1) * SUB] * decay
                weights.append((jnp.where(causal, weight, 0.0) if i == j else weight).astype(BF16))
            total = held[rows, cols] + skip_ref[:, cols] * x_now.astype(F32)
            total = total + dot(jnp.concatenate(weights, 1), jnp.concatenate(stacked, 0))
            total = total * silu(gate_ref[rows, cols].astype(F32))
            held[rows, cols] = total
            squares[i] = squares[i] + total * total

    def store(out_ref):
        for i in range(subs):
            rows = slice(i * SUB, (i + 1) * SUB)
            mean = jnp.sum(squares[i], axis=1, keepdims=True) * (1.0 / width)
            inverse = lax.rsqrt(mean + EPSILON)
            for p in range(tiles):
                cols = slice(p * LANES, (p + 1) * LANES)
                out_ref[rows, cols] = (held[rows, cols] * inverse * gain_ref[:, cols]).astype(BF16)

    if near:
        pl.when(pl.program_id(0) < near)(lambda: store(rest[-4]))
        pl.when(pl.program_id(0) >= near)(lambda: store(rest[-3]))
    else:
        store(rest[-3])


def outputs(group, groups, q, far, first, count, span, me, conved, logs, enter, gate, gain,
            token=None, target=None):
    xc, mc, local = conved
    split, spread_log, rel, before, reach, skip = logs
    _, width = xc.shape
    heads = before.shape[1]
    blocks = span // q
    home = target is not None and far > 0
    own = target is not None and far == 0

    def at(i, s):
        if home:
            return (s[0] ^ jnp.where(i < blocks, 1, 0)) * blocks + lax.rem(i, blocks)
        return (s[0] ^ far) * blocks + first + i

    in_specs = [
        pl.BlockSpec((q, width), lambda i, s: (at(i, s), 0)),
        pl.BlockSpec((q, 2 * STATE), lambda i, s: (at(i, s), 0)),
        pl.BlockSpec((q, width), lambda i, s: (at(i, s), group)),
        pl.BlockSpec((q, 4 * heads), lambda i, s: (at(i, s), 0)),
        pl.BlockSpec((1, q // SUB, heads // 2, LANES), lambda i, s: (at(i, s), 0, 0, 0)),
        pl.BlockSpec((q, 4 * heads), lambda i, s: (at(i, s), 0)),
        pl.BlockSpec((1, 1, width), lambda i, s: (at(i, s), 0, group)),
        pl.BlockSpec((1, STATE, width), lambda i, s: (at(i, s), 0, 0)),
        whole((STATE, width)),
        whole((3 * width // HEAD_DIM, width)),
        pl.BlockSpec((1, width), lambda i, s: (0, group)),
        pl.BlockSpec((1, width), lambda i, s: (0, group)),
    ]
    operands = [
        xc, mc, gate, split, rel, spread_log, reach, local,
        enter, choice(heads // groups), gain, skip,
    ]
    if token is not None:
        in_specs.append(pl.BlockSpec(memory_space=pl.ANY))
        operands.append(token)
    aliases = {}
    if home or own:
        start = blocks if home else 0
        count = start + blocks
        out_shape, out_specs = [], []
        if home:
            out_shape.append(jax.ShapeDtypeStruct((span, width), BF16))
            out_specs.append(pl.BlockSpec((q, width), lambda i, s: (jnp.minimum(i, blocks - 1), 0)))
        out_specs.append(
            pl.BlockSpec((q, width), lambda i, s: (jnp.maximum(i - start, 0), s[0] * groups + group))
        )
        if isinstance(target, tuple):
            out_shape.append(jax.ShapeDtypeStruct(target, BF16))
        else:
            out_shape.append(jax.ShapeDtypeStruct(target.shape, BF16))
            in_specs.append(pl.BlockSpec(memory_space=pl.ANY))
            operands.append(target)
            aliases = {len(operands): len(out_shape) - 1}
    else:
        out_shape = jax.ShapeDtypeStruct((count * q, width), BF16)
        out_specs = pl.BlockSpec((q, width), lambda i, s: (i, 0))
    return pl.pallas_call(
        functools.partial(outputs_kernel, group, blocks if home else 0),
        grid_spec=pltpu.PrefetchScalarGridSpec(
            num_scalar_prefetch=1,
            grid=(count,),
            in_specs=in_specs,
            out_specs=out_specs,
            scratch_shapes=[pltpu.VMEM((q, width), F32)] * 2,
        ),
        out_shape=out_shape,
        input_output_aliases=aliases,
        compiler_params=params(1),
        cost_estimate=cost(
            count * q * width * (2 * STATE + 4 * q), 8 * count * q * width, count * q * width * 4
        ),
        name="outputs",
    )(me, *operands)


def place_kernel(places, width, me_ref, *refs):
    count = len(places)
    out_ref, held, taken, put = refs[count + 1 :]
    copies = []
    at = 0
    for i, (far, group, groups, first, rows) in enumerate(places):
        slot = held.at[pl.ds(at, rows), :]
        column = pl.multiple_of(((me_ref[0] ^ far) * groups + group) * width, width)
        into = out_ref.at[pl.ds(first, rows), pl.ds(column, width)]
        copies.append(
            (
                pltpu.make_async_copy(refs[i], slot, taken.at[i]),
                pltpu.make_async_copy(slot, into, put.at[i]),
            )
        )
        at += rows
    for take, _ in copies:
        take.start()
    for take, give in copies:
        take.wait()
        give.start()
    for _, give in copies:
        give.wait()


def place(target, blocks, places, me):
    width = blocks[0].shape[1]
    total = sum(block.shape[0] for block in blocks)
    count = len(blocks)
    return pl.pallas_call(
        functools.partial(place_kernel, places, width),
        in_specs=[pl.BlockSpec(memory_space=pltpu.SMEM)]
        + [pl.BlockSpec(memory_space=pl.ANY)] * (count + 1),
        out_specs=pl.BlockSpec(memory_space=pl.ANY),
        out_shape=jax.ShapeDtypeStruct(target.shape, target.dtype),
        scratch_shapes=[
            pltpu.VMEM((total, width), BF16),
            pltpu.SemaphoreType.DMA((count,)),
            pltpu.SemaphoreType.DMA((count,)),
        ],
        input_output_aliases={count + 1: 0},
        compiler_params=pltpu.CompilerParams(vmem_limit_bytes=SMALL_LIMIT),
        cost_estimate=cost(0, 4 * total * width),
        name="place",
    )(me, *blocks, target)


def per_device(
    channels_in,
    state_maps,
    gate_in,
    step_raw,
    convolution_channel_taps,
    conv_maps,
    head_rates,
    skip_gain,
    norm_gain,
):
    rows, channels = channels_in.shape
    heads = step_raw.shape[1]
    map_width = state_maps.shape[2]
    groups = map_width // STATE
    width = heads // groups * HEAD_DIM
    shards = lax.axis_size("ctx")
    peers = lax.axis_size("head")
    me = lax.axis_index("head").reshape(1)
    span = rows // peers
    q = LANES if span % LANES == 0 else HEAD_DIM

    maps = state_maps.reshape(rows, 2 * map_width)
    ahead = [(i, i + 1) for i in range(shards - 1)]
    edge = jnp.concatenate([channels_in[rows - 8 :], maps[rows - 8 :]], 1)
    halo = lax.ppermute(edge, "ctx", ahead)

    logs = prep(step_raw, head_rates, skip_gain, q, groups)
    gain = norm_gain[None, :]

    def shard_states(group):
        blocks = rows // q
        cuts = [0, blocks] if group == 0 else [0, blocks // 2, blocks]
        done = None
        for first, last in zip(cuts[:-1], cuts[1:]):
            done = states(
                group, groups, shards, q, first, last, channels_in, maps, halo,
                convolution_channel_taps, conv_maps, logs[1], logs[3], done,
            )
        return done[:3], done[3].reshape(shards, STATE // shards, width + LANES)

    def exchange(payload):
        return lax.all_to_all(payload, "ctx", 0, 0, tiled=True)

    def block_of(group, far, first, count, **more):
        return outputs(
            group, groups, q, far, first, count, span, me, conved[group], logs, entering[group],
            gate_in, gain, **more,
        )

    def send(block, far):
        return lax.ppermute(block, "head", [(i, i ^ far) for i in range(peers)])

    conved, payloads = zip(*[shard_states(group) for group in range(groups)])
    entering, arrived, tokens = [], [], []
    blocks = span // q
    result = (span, channels * peers)
    for group in range(groups):
        payload = payloads[group]
        if group > 0:
            payload, _ = lax.optimization_barrier((payload, tokens[0]))
        part = exchange(payload)
        part = scan_shards(part)
        entering.append(exchange(part).reshape(STATE, width))
        for far in range(peers - 1, 1, -1):
            for first, last in sends(group, groups, far, peers, blocks):
                block = block_of(
                    group, far, first, last - first, token=tokens[-1] if tokens else None
                )
                tokens.append(block)
                arrived.append((send(block, far), (far, group, groups, first * q, (last - first) * q)))
        if group < groups - 1:
            home = block_of(group, 1, 0, blocks, token=tokens[-1])
            arrived.append((send(home, 1), (1, group, groups, 0, span)))
    for group in range(groups):
        if group < groups - 1:
            (result,) = block_of(group, 0, 0, blocks, token=tokens[-1], target=result)
        else:
            home, result = block_of(group, 1, 0, blocks, token=tokens[-1], target=result)
    arrived.append((send(home, 1), (1, groups - 1, groups, 0, span)))
    arrived.sort(key=lambda a: (a[1][1] == groups - 1 and a[1][0] > 1))
    late = sum(a[1][1] == groups - 1 and a[1][0] > 1 for a in arrived)
    cuts = [0, len(arrived) - late, len(arrived) - 1, len(arrived)]
    for low, high in zip(cuts[:-1], cuts[1:]):
        if high > low:
            part = arrived[low:high]
            result = place(result, [a[0] for a in part], [a[1] for a in part], me)
    return result


def sends(group, groups, far, peers, blocks):
    if blocks > 1 and groups > 1 and group == 0 and far == peers - 1:
        return [(0, blocks - 1), (blocks - 1, blocks)]
    if blocks > 1 and far == peers - 1:
        return [(0, 1), (1, blocks)]
    if blocks > 1 and group == groups - 1 and far == 2:
        return [(0, blocks - 1), (blocks - 1, blocks)]
    return [(0, blocks)]


def solution(mesh):
    return jax.shard_map(
        per_device,
        mesh=mesh,
        in_specs=(
            P("ctx", "head"),
            P("ctx", None, "head"),
            P("ctx", "head"),
            P("ctx", "head"),
            P(None, "head"),
            P(None, None, "head"),
            P(None, "head"),
            P("head"),
            P("head"),
        ),
        out_specs=P(("ctx", "head"), None),
        check_vma=False,
    )
```
